32 devices in a mesh: dp: 4 (over y, core), seq: 8 (over z, x).
Axes of the slice: x: 2, y: 2, z: 4, core: 2. Of those that a mesh axis runs over, the one named last changes fastest.
Arguments:
- tokens: bfloat16 [4, 1024, 4096], P('dp', 'seq'), may hold values from -32 to 32
- projection: bfloat16 [4096, 3, 32, 128], P(None, None, 'seq'), may hold values from -1 to 1
- flow_lengths: int32 [4, 6], P('dp'), may hold values from 1 to 2, 8 in all within a row
- flow_owner: int32 [4, 8], P('dp'), may hold values from 0 to 7, each once within a row
- tile_mask: int32 [4, 8, 1], P('dp'), may hold values 0 or 1
- cotangent: bfloat16 [4, 16, 128, 4096], P('dp', 'seq'), may hold values from -1.5 to 1.5
Outputs:
- attended: bfloat16 [4, 16, 128, 4096], P('dp', 'seq')
- projection_grad: float32 [4096, 3, 32, 128], P(None, None, 'seq')
The draws below stay inside these ranges and needn't reach their ends.
Inputs may be any that keep to these rules, and one draw needn't show every extreme that they name: `flow_lengths`: in each group the lengths add up to 8, and at least one flow has exactly 2 tiles. Each row is a permutation; flow f < 6 goes to owner flow_owner[g, f], the other entries name owners without a flow.
All inputs are finite; a program needn't handle non-finite values. No bound on the sum of `tile_mask` on one device may be relied on, other than what follows from the above.
Results may differ from the reference program's by a relative error of at most 0.013.
Values may be sent and summed in bfloat16 or wider, within the bound.
A program may use at most 192 MiB of HBM per device.

```python
import math
import jax
import jax.numpy as jnp
import numpy as np
from jax import lax

D = 4096
HEADS = 32
HD = 128
TILE = 128
CAP = 2
TILES = 8
TOKENS = 1024
FLOWS = 6
SLOTS = 16
GROUPS = 4
N_SEQ = 8


def draw_tokens(key, part):
    first_key = jax.random.fold_in(key, 0)
    sampled = jnp.clip(jax.random.normal(first_key, (GROUPS, TOKENS, D), jnp.float32), -6.0, 6.0)
    return sampled.astype(jnp.bfloat16)


def draw_projection(key, part):
    first_key = jax.random.fold_in(key, 0)
    matrix = jnp.clip(jax.random.normal(first_key, (D, 3, HEADS, HD), jnp.float32), -6.0, 6.0) * D ** (-0.5)
    return matrix.astype(jnp.bfloat16)


def with_ends(array, rng, low, top_value):
    index_at = [jax.random.randint(jax.random.fold_in(rng, axis), (), 0, length) for axis, length in enumerate(array.shape)]
    longest = array.shape.index(max(array.shape))
    beside = index_at[:longest] + [(index_at[longest] + 1) % array.shape[longest]] + index_at[longest + 1:]
    return array.at[tuple(index_at)].set(low).at[tuple(beside)].set(top_value)


def block_levels(key, shape, shards, low, largest):
    def one(dim, shards_of):
        draws = jax.random.uniform(jax.random.fold_in(jax.random.fold_in(key, 6), dim), (shards_of,), jnp.float32, low / len(shards), largest / len(shards))
        return jnp.repeat(jnp.exp(draws), shape[dim] // shards_of).reshape((-1,) + (1,) * (len(shape) - dim - 1))

    level = one(*shards[0])
    for cut in shards[1:]:
        level = level * one(*cut)
    return level


def profile(amount, total, reach, slope):
    weights = [(1 << 20) // math.isqrt(standing ** slope) + 1 for standing in range(2, amount + 1)]
    surplus, counts = total - reach - (amount - 1), [1] * (amount - 1)
    while surplus > 0:
        candidates = [i for i in range(amount - 1) if counts[i] < reach]
        whole, budget = sum([weights[i] for i in candidates]), surplus
        for i in candidates:
            extra = min(reach - counts[i], max(1, budget * weights[i] // whole), surplus)
            counts[i] = counts[i] + extra
            surplus = surplus - extra
    return np.array([reach] + counts)


def ragged(key, amount, total, limit, skew):
    if amount == 2:
        one = jax.random.randint(key, (), max(1, total - limit), min(limit, total - 1) + 1)
        return jnp.stack([one, total - one])
    lengths = jnp.asarray(profile(amount, total, limit, skew), jnp.int32)
    twos = (amount - 1) // 2
    source_of, sink = lengths[1:1 + 2 * twos:2], lengths[2:2 + 2 * twos:2]
    margin = jnp.minimum(source_of - 1, limit - sink)
    passed = jax.random.randint(jax.random.fold_in(key, 1), (twos,), 0, 1 << 20) % (margin + 1)
    lengths = lengths.at[1:1 + 2 * twos:2].set(source_of - passed).at[2:2 + 2 * twos:2].set(sink + passed)
    return lengths[jax.random.permutation(jax.random.fold_in(key, 2), amount)]


def centred(own_key, extent, width, reach, shards=(), held_as=jnp.bfloat16):
    drawn = width * jax.random.normal(own_key, extent, jnp.float32)
    if shards:
        drawn = drawn * block_levels(own_key, extent, shards, -0.22, 0.18)
    return jnp.clip(drawn, -reach, reach).astype(held_as)


def setup_inputs(seed: int = 0) -> dict:
    keys = jax.random.split(jax.random.key(seed), 7)
    return {
        "tokens": draw_tokens(jax.random.fold_in(keys[6], 71), 0),
        "projection": draw_projection(jax.random.fold_in(keys[6], 71), 0),
        "flow_lengths": jax.vmap(lambda own: ragged(own, FLOWS, TILES, CAP, 2))(jax.random.split(keys[2], GROUPS)).reshape((GROUPS, FLOWS)).astype(jnp.int32),
        "flow_owner": jax.vmap(lambda own: jax.random.permutation(own, N_SEQ))(jax.random.split(keys[3], GROUPS)).reshape((GROUPS, N_SEQ)).astype(jnp.int32),
        "tile_mask": with_ends((jax.random.randint(keys[4], (GROUPS, TILES, CAP - 1), 0, 4) < 3).astype(jnp.int32), jax.random.fold_in(keys[4], 1), 0, 1),
        "cotangent": centred(keys[5], (GROUPS, SLOTS, TILE, HEADS * HD), 0.25, 1.5, ((0, 4), (1, 8))),
    }


def tile_plan(flow_sizes, owner_row, tile_count, flow_count):
    flow_starts = (jnp.cumsum(flow_sizes) - flow_sizes).astype(jnp.int32)
    tile_ids = jnp.arange(tile_count, dtype=jnp.int32)
    flow_index = jnp.sum((flow_starts[None, :] <= tile_ids[:, None]).astype(jnp.int32), axis=1) - 1
    onehot = (flow_index[:, None] == jnp.arange(flow_count, dtype=jnp.int32)[None, :]).astype(jnp.int32)
    position = (tile_ids - jnp.sum(onehot * flow_starts[None, :], axis=1)).astype(jnp.int32)
    tile_owner = jnp.sum(onehot * owner_row[None, :flow_count], axis=1).astype(jnp.int32)
    return position, tile_owner


def visibility(position, tile_marks, span):
    columns = [jnp.ones(position.shape, dtype=bool)]
    for offset in range(1, span):
        columns.append((position >= offset) & (tile_marks[:, offset - 1] == 1))
    return jnp.stack(columns, axis=1)


def windows(key_tiles, span):
    pieces = [key_tiles]
    for offset in range(1, span):
        padding = jnp.zeros((offset,) + key_tiles.shape[1:], key_tiles.dtype)
        pieces.append(jnp.concatenate([padding, key_tiles[:-offset]], axis=0))
    return jnp.stack(pieces, axis=1)


def unwindow(grad_win, span):
    summed = grad_win[:, 0]
    for offset in range(1, span):
        padding = jnp.zeros((offset,) + summed.shape[1:], summed.dtype)
        summed = summed + jnp.concatenate([grad_win[offset:, offset], padding], axis=0)
    return summed


def attend(queries, key_win, value_win, visible, score_scale):
    scores = jnp.einsum('bthe,bwshe->bhtws', queries.astype(jnp.float32), key_win.astype(jnp.float32)) * score_scale
    scores = jnp.where(visible[:, None, None, :, None], scores, jnp.float32(-1e30))
    row_max = jnp.max(scores, axis=(3, 4), keepdims=True)
    raised = jnp.exp(scores - row_max)
    soft_weights = raised / jnp.sum(raised, axis=(3, 4), keepdims=True)
    soft_half = soft_weights.astype(jnp.bfloat16)
    outputs = jnp.einsum('bhtws,bwshe->bthe', soft_half.astype(jnp.float32), value_win.astype(jnp.float32)).astype(jnp.bfloat16)
    return outputs, soft_weights, soft_half


def attend_back(queries, key_win, value_win, soft_weights, soft_half, grad_out, score_scale, span):
    grad_probs = jnp.einsum('bthe,bwshe->bhtws', grad_out.astype(jnp.float32), value_win.astype(jnp.float32))
    correction = jnp.sum(soft_weights * grad_probs, axis=(3, 4), keepdims=True)
    grad_scores = (soft_weights * (grad_probs - correction) * score_scale).astype(jnp.bfloat16)
    grad_query = jnp.einsum('bhtws,bwshe->bthe', grad_scores.astype(jnp.float32), key_win.astype(jnp.float32)).astype(jnp.bfloat16)
    grad_key_win = jnp.einsum('bhtws,bthe->bwshe', grad_scores.astype(jnp.float32), queries.astype(jnp.float32))
    grad_value_win = jnp.einsum('bhtws,bthe->bwshe', soft_half.astype(jnp.float32), grad_out.astype(jnp.float32))
    grad_key = unwindow(grad_key_win, span).astype(jnp.bfloat16)
    grad_value = unwindow(grad_value_win, span).astype(jnp.bfloat16)
    return grad_query, grad_key, grad_value


def reference(tokens, projection, flow_lengths, flow_owner, tile_mask, cotangent):
    flat_weight = projection.reshape(D, 3 * HEADS * HD)
    score_scale = HD ** -0.5

    def one_group(grad_total, inputs):
        token_rows, flow_sizes, owner_row, tile_marks, group_cot = inputs
        projected = jnp.dot(token_rows, flat_weight, preferred_element_type=jnp.float32).astype(jnp.bfloat16)
        projected = projected.reshape(TILES, TILE, 3, HEADS, HD)
        queries = projected[:, :, 0]
        key_tiles = projected[:, :, 1]
        value_tiles = projected[:, :, 2]
        position, tile_owner = tile_plan(flow_sizes, owner_row, TILES, FLOWS)
        visible = visibility(position, tile_marks, CAP)
        key_win = windows(key_tiles, CAP)
        value_win = windows(value_tiles, CAP)
        outputs, soft_weights, soft_half = attend(queries, key_win, value_win, visible, score_scale)
        slot_index = tile_owner * CAP + position
        packed = jnp.zeros((SLOTS, TILE, HEADS * HD), jnp.bfloat16).at[slot_index].set(outputs.reshape(TILES, TILE, HEADS * HD))
        grad_out = group_cot[slot_index].reshape(TILES, TILE, HEADS, HD)
        grad_query, grad_key, grad_value = attend_back(queries, key_win, value_win, soft_weights, soft_half, grad_out, score_scale, CAP)
        grad_proj = jnp.stack([grad_query, grad_key, grad_value], axis=2).reshape(TOKENS, 3 * HEADS * HD)
        partial_value = lax.dot_general(token_rows, grad_proj, (((0,), (0,)), ((), ())), preferred_element_type=jnp.float32)
        rounded = lax.optimization_barrier(partial_value.astype(jnp.bfloat16)).astype(jnp.float32)
        return grad_total + rounded, packed

    start_grad = jnp.zeros((D, 3 * HEADS * HD), jnp.float32)
    grad_total, packed = lax.scan(one_group, start_grad, (tokens, flow_lengths, flow_owner, tile_mask, cotangent))
    return packed, grad_total.reshape(D, 3, HEADS, HD)
```

```python
import functools

import jax
import jax.numpy as jnp
from jax import lax
from jax.experimental import pallas as pl
from jax.experimental.pallas import tpu as pltpu
from jax.sharding import PartitionSpec as P

TILE = 128
CAP = 2
MESH = pl.DeviceIdType.MESH
CHUNKS = 8
PARTS = 2


def tile_plan(flow_sizes, owner_row, tile_count, flow_count):
    flow_starts = jnp.cumsum(flow_sizes) - flow_sizes
    tile_ids = jnp.arange(tile_count, dtype=jnp.int32)
    flow_index = jnp.sum((flow_starts[None, :] <= tile_ids[:, None]).astype(jnp.int32), axis=1) - 1
    onehot = (flow_index[:, None] == jnp.arange(flow_count, dtype=jnp.int32)[None, :]).astype(
        jnp.int32
    )
    position = tile_ids - jnp.sum(onehot * flow_starts[None, :], axis=1)
    tile_owner = jnp.sum(onehot * owner_row[None, :flow_count], axis=1)
    return (position, tile_owner, flow_starts)


def visibility(position, tile_marks):
    columns = [jnp.ones(position.shape, dtype=bool)]
    columns.append((position >= 1) & (tile_marks[:, 0] == 1))
    return jnp.stack(columns, axis=1)


def windows(key_tiles):
    pieces = [key_tiles]
    padding = jnp.zeros((1,) + key_tiles.shape[1:], key_tiles.dtype)
    pieces.append(jnp.concatenate([padding, key_tiles[:-1]], axis=0))
    return jnp.stack(pieces, axis=1)


def unwindow(grad_win):
    summed = grad_win[:, 0]
    padding = jnp.zeros((1,) + summed.shape[1:], summed.dtype)
    summed = summed + jnp.concatenate([grad_win[1:, 1], padding], axis=0)
    return summed


def attend(queries, key_win, value_win, visible, score_scale):
    scores = (
        jnp.einsum("bthe,bwshe->bhtws", queries, key_win, preferred_element_type=jnp.float32)
        * score_scale
    )
    scores = jnp.where(visible[:, None, None, :, None], scores, jnp.float32(-1e30))
    row_max = jnp.max(scores, axis=(3, 4), keepdims=True)
    raised = jnp.exp(scores - row_max)
    soft_weights = raised / jnp.sum(raised, axis=(3, 4), keepdims=True)
    soft_half = soft_weights.astype(jnp.bfloat16)
    outputs = jnp.einsum(
        "bhtws,bwshe->bthe", soft_half, value_win, preferred_element_type=jnp.float32
    ).astype(jnp.bfloat16)
    return (outputs, soft_weights, soft_half)


def attend_back(queries, key_win, value_win, soft_weights, soft_half, grad_out, score_scale):
    grad_probs = jnp.einsum(
        "bthe,bwshe->bhtws", grad_out, value_win, preferred_element_type=jnp.float32
    )
    correction = jnp.sum(soft_weights * grad_probs, axis=(3, 4), keepdims=True)
    grad_scores = (soft_weights * (grad_probs - correction) * score_scale).astype(jnp.bfloat16)
    grad_query = jnp.einsum(
        "bhtws,bwshe->bthe", grad_scores, key_win, preferred_element_type=jnp.float32
    ).astype(jnp.bfloat16)
    grad_key_win = jnp.einsum(
        "bhtws,bthe->bwshe", grad_scores, queries, preferred_element_type=jnp.float32
    )
    grad_value_win = jnp.einsum(
        "bhtws,bthe->bwshe", soft_half, grad_out, preferred_element_type=jnp.float32
    )
    grad_key = unwindow(grad_key_win).astype(jnp.bfloat16)
    grad_value = unwindow(grad_value_win).astype(jnp.bfloat16)
    return (grad_query, grad_key, grad_value)


def over_x(z, block_z, part):
    along = ((z == 0) & (block_z == 3) & (part == 1)) | ((z == 3) & (block_z == 0) & (part == 1))
    along = along | ((z == 1) & (block_z == 0)) | ((z == 2) & (block_z == 3))
    return jnp.logical_not(along)


def gather_kernel(tok_ref, out_ref, stage, up_sem, down_sem, x_sem, recv_sem, local_sem):
    me = lax.axis_index("seq")
    dp = lax.axis_index("dp")
    z, x = me // 2, me % 2
    rows = tok_ref.shape[0] // PARTS
    up, down, across = me + 2, me - 2, z * 2 + 1 - x

    barrier = pltpu.get_barrier_semaphore()

    def greet(target):
        pl.semaphore_signal(barrier, inc=1, device_id=(dp, target), device_id_type=MESH)

    greet(across)
    pl.when(z < 3)(lambda: greet(up))
    pl.when(z > 0)(lambda: greet(down))
    inner = (z + 1) // 2 % 2
    pl.semaphore_wait(barrier, 2 + inner)

    def copy(block, part, target, send_sem, own):
        piece = pl.ds(part * rows, rows)
        source = tok_ref.at[piece] if own else out_ref.at[block, piece]
        return pltpu.make_async_remote_copy(
            src_ref=source,
            dst_ref=out_ref.at[block, piece],
            send_sem=send_sem.at[block, part],
            recv_sem=recv_sem.at[block, part],
            device_id=(dp, target),
            device_id_type=MESH,
        )

    def routes(block_z, same, part):
        if same:
            return (
                ((z < 3) & (block_z <= z), up, up_sem),
                ((z > 0) & (block_z >= z), down, down_sem),
                (over_x(z, block_z, part), across, x_sem),
            )
        return (
            ((z < 3) & (block_z <= z) & jnp.logical_not(over_x(z + 1, block_z, part)), up, up_sem),
            (
                (z > 0) & (block_z >= z) & jnp.logical_not(over_x(z - 1, block_z, part)),
                down,
                down_sem,
            ),
        )

    def each(block_z, same, part, own, act):
        block = block_z * 2 + (x if same else 1 - x)
        for condition, target, sem in routes(block_z, same, part):

            @pl.when(condition)
            def _():
                act(copy(block, part, target, sem, own))

    for part in range(PARTS):
        each(z, True, part, True, lambda c: c.start())
    fetch = pltpu.make_async_copy(tok_ref, stage, local_sem.at[0])
    fetch.start()
    fetch.wait()
    put = pltpu.make_async_copy(stage, out_ref.at[me], local_sem.at[1])
    put.start()

    order = []
    for distance in (1, 2, 3):
        for sign in (-1, 1):
            order.append((sign * distance, True))
        if distance == 1:
            order.append((0, False))
        else:
            for sign in (-1, 1):
                order.append((sign * (distance - 1), False))
    order += [(-3, False), (3, False)]

    for shift, same in order:
        block_z = z + shift
        valid = (block_z >= 0) & (block_z <= 3)
        block = block_z * 2 + (x if same else 1 - x)

        @pl.when(valid)
        def _():
            for part in range(PARTS):
                copy(block, part, across, x_sem, False).wait_recv()
                each(block_z, same, part, False, lambda c: c.start())

    put.wait()
    for part in range(PARTS):
        each(z, True, part, True, lambda c: c.wait_send())
    for shift, same in order:
        block_z = z + shift

        @pl.when((block_z >= 0) & (block_z <= 3))
        def _():
            for part in range(PARTS):
                each(block_z, same, part, False, lambda c: c.wait_send())


def gather_tokens(token_rows, seq_count):
    rows, width = token_rows.shape
    sems = pltpu.SemaphoreType.DMA((seq_count, PARTS))
    out = pl.pallas_call(
        gather_kernel,
        out_shape=jax.ShapeDtypeStruct((seq_count, rows, width), token_rows.dtype),
        in_specs=[pl.BlockSpec(memory_space=pl.ANY)],
        out_specs=pl.BlockSpec(memory_space=pl.ANY),
        scratch_shapes=[
            pltpu.VMEM((rows, width), token_rows.dtype),
            sems,
            sems,
            sems,
            sems,
            pltpu.SemaphoreType.DMA((2,)),
        ],
        compiler_params=pltpu.CompilerParams(collective_id=1, has_side_effects=True),
        cost_estimate=pl.CostEstimate(flops=0, bytes_accessed=300_000_000, transcendentals=0),
    )(token_rows)
    return out.reshape(seq_count * rows, width)


def reduce_kernel(
    tok_ref, grad_ref, total_ref, keep, send, got, other, a_send, a_recv, b_send, b_recv, c_send, c_recv
):
    dp = lax.axis_index("dp")
    seq = lax.axis_index("seq")
    core, y = dp % 2, dp // 2
    mate = (y * 2 + 1 - core, seq)
    far = ((1 - y) * 2 + core, seq)
    half = keep.shape[1]

    barrier = pltpu.get_barrier_semaphore()
    for peer in (mate, far):
        pl.semaphore_signal(barrier, inc=1, device_id=peer, device_id_type=MESH)
    pl.semaphore_wait(barrier, 2)

    def remote(src, dst, send_sem, recv_sem, peer):
        return pltpu.make_async_remote_copy(
            src_ref=src,
            dst_ref=dst,
            send_sem=send_sem,
            recv_sem=recv_sem,
            device_id=peer,
            device_id_type=MESH,
        )

    def to_mate(i):
        return remote(send.at[i], got.at[i], a_send.at[i], a_recv.at[i], mate)

    def to_far(i):
        return remote(keep.at[i], other.at[i], b_send.at[i], b_recv.at[i], far)

    def share(i, side):
        spot = total_ref.at[i, side]
        return remote(spot, spot, c_send.at[i], c_recv.at[i], mate)

    def product(i, side):
        columns = pl.ds(pl.multiple_of((i * 2 + side) * half, half), half)
        return lax.dot_general(
            tok_ref[:, columns],
            grad_ref[...],
            (((0,), (0,)), ((), ())),
            preferred_element_type=jnp.float32,
        ).astype(jnp.bfloat16)

    def pass_on(i):
        to_mate(i).wait_recv()
        keep[i] = (keep[i].astype(jnp.float32) + got[i].astype(jnp.float32)).astype(jnp.bfloat16)
        to_far(i).start()

    def first(i, carry):
        send[i] = product(i, 1 - core)
        to_mate(i).start()
        keep[i] = product(i, core)

        @pl.when(i > 0)
        def _():
            pass_on(i - 1)

        return carry

    lax.fori_loop(0, CHUNKS, first, 0)
    pass_on(CHUNKS - 1)

    def second(i, carry):
        to_far(i).wait_recv()
        total_ref[i, core] = (
            keep[i].astype(jnp.float32) + other[i].astype(jnp.float32)
        ).astype(jnp.bfloat16)
        share(i, core).start()
        return carry

    lax.fori_loop(0, CHUNKS, second, 0)

    def finish(i, carry):
        share(i, 1 - core).wait_recv()
        share(i, core).wait_send()
        to_mate(i).wait_send()
        to_far(i).wait_send()
        return carry

    lax.fori_loop(0, CHUNKS, finish, 0)


def reduced_grad(gathered, grad_proj):
    tokens, width = gathered.shape
    columns = grad_proj.shape[1]
    half = width // CHUNKS // 2
    block = pltpu.VMEM((CHUNKS, half, columns), jnp.bfloat16)
    sems = pltpu.SemaphoreType.DMA((CHUNKS,))
    vmem = pl.BlockSpec(memory_space=pltpu.VMEM)
    total = pl.pallas_call(
        reduce_kernel,
        out_shape=jax.ShapeDtypeStruct((CHUNKS, 2, half, columns), jnp.bfloat16),
        in_specs=[vmem, vmem],
        out_specs=vmem,
        scratch_shapes=[block] * 4 + [sems] * 6,
        compiler_params=pltpu.CompilerParams(
            collective_id=2, has_side_effects=True, vmem_limit_bytes=63 * 1024 * 1024
        ),
        cost_estimate=pl.CostEstimate(
            flops=2 * tokens * width * columns, bytes_accessed=500_000_000, transcendentals=0
        ),
    )(gathered, grad_proj)
    return total.reshape(width, columns)


def widen_kernel(in_ref, out_ref):
    rows, columns = in_ref.shape
    lanes = out_ref.shape[1]
    count = columns // lanes
    for j in range(count):
        out_ref[pl.ds(j, rows, stride=count), :] = in_ref[:, j * lanes : (j + 1) * lanes].astype(
            jnp.float32
        )


def widen(total, head_size):
    width, columns = total.shape
    rows = 256
    count = columns // head_size
    return pl.pallas_call(
        widen_kernel,
        grid=(width // rows,),
        out_shape=jax.ShapeDtypeStruct((width * count, head_size), jnp.float32),
        in_specs=[pl.BlockSpec((rows, columns), lambda i: (i, 0))],
        out_specs=pl.BlockSpec((rows * count, head_size), lambda i: (i, 0)),
    )(total)


def shards(fast, tokens, projection, flow_lengths, flow_owner, tile_mask, cotangent):
    token_rows = tokens[0]
    model_width, triple, heads_here, head_size = projection.shape
    width_here = heads_here * head_size
    seq_count = lax.axis_size("seq")
    my_index = lax.axis_index("seq")
    local_cot = cotangent[0].reshape(CAP, TILE, seq_count, width_here)
    flat_weight = projection.reshape(model_width, triple * width_here)
    spread_back = lax.all_to_all(local_cot, "seq", split_axis=2, concat_axis=2, tiled=True)
    if fast:
        token_rows, spread_back, flat_weight = lax.optimization_barrier(
            (token_rows, spread_back, flat_weight)
        )
        gathered = gather_tokens(token_rows, seq_count)
    else:
        gathered = lax.all_gather(token_rows, "seq", axis=0, tiled=True)
    projected = jnp.dot(gathered, flat_weight, preferred_element_type=jnp.float32).astype(
        jnp.bfloat16
    )
    tile_count = gathered.shape[0] // TILE
    flow_sizes = flow_lengths[0]
    owner_row = flow_owner[0]
    tile_marks = tile_mask[0]
    flow_count = flow_sizes.shape[0]
    position, tile_owner, flow_starts = tile_plan(flow_sizes, owner_row, tile_count, flow_count)
    owner_match = (
        owner_row[None, :flow_count] == jnp.arange(seq_count, dtype=jnp.int32)[:, None]
    ).astype(jnp.int32)
    own_start = jnp.sum(owner_match * flow_starts[None, :], axis=1)
    own_size = jnp.sum(owner_match * flow_sizes[None, :], axis=1)
    slot_ids = jnp.arange(CAP, dtype=jnp.int32)
    pick_tile = jnp.clip(own_start[None, :] + slot_ids[:, None], 0, tile_count - 1)
    my_hit = jnp.arange(seq_count, dtype=jnp.int32) == my_index
    my_size = jnp.sum(jnp.where(my_hit, own_size, 0))
    slot_valid = slot_ids < my_size
    score_scale = head_size ** (-0.5)
    projected_tiles = projected.reshape(tile_count, TILE, triple, width_here)
    within = jnp.arange(TILE, dtype=jnp.int32)
    queries = projected_tiles[:, :, 0].reshape(tile_count, TILE, heads_here, head_size)
    key_win = windows(projected_tiles[:, :, 1].reshape(tile_count, TILE, heads_here, head_size))
    value_win = windows(projected_tiles[:, :, 2].reshape(tile_count, TILE, heads_here, head_size))
    visible = visibility(position, tile_marks)
    outputs, soft_weights, soft_half = attend(queries, key_win, value_win, visible, score_scale)
    flat_out = outputs.reshape(tile_count, TILE, width_here)
    send_buffer = flat_out[pick_tile[:, None, :], within[None, :, None]]
    received = lax.all_to_all(send_buffer, "seq", split_axis=2, concat_axis=2, tiled=True)
    packed = jnp.where(
        slot_valid[:, None, None],
        received.reshape(CAP, TILE, seq_count * width_here),
        jnp.zeros((), jnp.bfloat16),
    )
    grad_out = spread_back[position[:, None], within[None, :], tile_owner[:, None]].reshape(
        tile_count, TILE, heads_here, head_size
    )
    grad_query, grad_key, grad_value = attend_back(
        queries, key_win, value_win, soft_weights, soft_half, grad_out, score_scale
    )
    grad_proj_tiles = jnp.stack([grad_query, grad_key, grad_value], axis=2).reshape(
        tile_count, TILE, triple, width_here
    )
    grad_proj = grad_proj_tiles.reshape(tile_count * TILE, triple * width_here)
    if fast:
        grad_total = widen(reduced_grad(gathered, grad_proj), head_size)
    else:
        partial_value = lax.dot_general(
            gathered, grad_proj, (((0,), (0,)), ((), ())), preferred_element_type=jnp.float32
        )
        grad_total = lax.psum(partial_value.astype(jnp.bfloat16), "dp").astype(jnp.float32)
    return (packed[None], grad_total.reshape(projection.shape))


def solution(mesh):
    placed = (
        P("dp", "seq", None),
        P(None, None, "seq", None),
        P("dp", None),
        P("dp", None),
        P("dp", None, None),
        P("dp", "seq", None, None),
    )
    fast = mesh.shape["dp"] == 4 and mesh.shape["seq"] == 8
    return jax.shard_map(
        functools.partial(shards, fast),
        mesh=mesh,
        in_specs=placed,
        out_specs=(P("dp", "seq", None, None), P(None, None, "seq", None)),
        check_vma=False,
    )
```
